32 devices in a mesh: row: 4 (over y, core), col: 8 (over z, x).
Axes of the slice: x: 2, y: 2, z: 4, core: 2. Of those that a mesh axis runs over, the one named last changes fastest.
Arguments:
- matrix: float32 [16384, 16384], P('row', 'col'), as said below
Outputs:
- updated: float32 [16384, 16384], P('row', 'col')
- reflectors: float32 [1, 16384, 256], P(None, ('row', 'col'))
- products: float32 [1, 16384, 256], P(None, ('row', 'col'))
Inputs may be any that keep to these rules, and one draw needn't show every extreme that they name: `matrix`: symmetric.
All inputs are finite; a program needn't handle non-finite values.
Results may differ from the reference program's by a relative error of at most 0.0003.
Values sent between devices are 32-bit elements; how exact they have to be, the bound alone decides.
A program may use at most 192 MiB of HBM per device.

```python
import math
import jax
import jax.numpy as jnp
from jax import lax

ORDER = 16384
NB = 256
PANELS = 1


def draw_matrix(key, part):
    noise_key = jax.random.fold_in(key, 11)
    block_key = jax.random.fold_in(key, 23)
    noise = jax.random.normal(noise_key, (ORDER, ORDER), jnp.float32)
    sym_part = (noise + noise.T) * 0.7071
    diag_scale = 2.0 * math.sqrt(ORDER)
    spread = 0.35 * diag_scale / math.sqrt(NB)
    blocks = jax.random.normal(block_key, (2, NB, NB), jnp.float32) * spread
    blocks = blocks + diag_scale * jnp.eye(NB, dtype=jnp.float32)[None, :, :]
    planted = jnp.zeros((ORDER, ORDER), jnp.float32)
    planted = planted.at[NB:2 * NB, 0:NB].set(blocks[0])
    planted = planted.at[2 * NB:3 * NB, NB:2 * NB].set(blocks[1])
    result = sym_part + planted + planted.T
    return result


def setup_inputs(seed: int = 0) -> dict:
    key_of = jax.random.split(jax.random.key(seed), 2)
    matrix = draw_matrix(jax.random.fold_in(key_of[1], 71), 0)
    return {"matrix": matrix}


def matmul(left, right):
    return jnp.dot(left.astype(jnp.float32), right.astype(jnp.float32), precision=lax.Precision.HIGHEST, preferred_element_type=jnp.float32)

def lu_signed(square):
    order_n = square.shape[0]
    all_ids = jnp.arange(order_n)

    def lu_step(pivot_idx, state):
        work_mat, sign_vec = state
        column = work_mat[:, pivot_idx]
        raw_pivot = column[pivot_idx]
        sign_now = jnp.where(raw_pivot >= 0, 1.0, -1.0)
        pivot_val = raw_pivot + sign_now
        lower_col = jnp.where(all_ids > pivot_idx, column / pivot_val, 0.0)
        upper_row = jnp.where(all_ids > pivot_idx, work_mat[pivot_idx, :], 0.0)
        work_mat = work_mat - lower_col[:, None] * upper_row[None, :]
        kept = jnp.where(all_ids > pivot_idx, lower_col, jnp.where(all_ids == pivot_idx, pivot_val, column))
        work_mat = work_mat.at[:, pivot_idx].set(kept)
        sign_vec = sign_vec.at[pivot_idx].set(sign_now)
        return (work_mat, sign_vec)
    packed, sign_vec = lax.fori_loop(0, order_n, lu_step, (square, jnp.zeros((order_n,), square.dtype)))
    unit_lower = jnp.tril(packed, -1) + jnp.eye(order_n, dtype=square.dtype)
    return (unit_lower, jnp.triu(packed), sign_vec)

def reference(matrix):
    row_ids = jnp.arange(matrix.shape[0])
    current = matrix
    all_refl = []
    all_prod = []
    for panel_idx in range(PANELS):
        col_start = panel_idx * NB
        row_start = col_start + NB
        panel_cols = jnp.where((row_ids >= row_start)[:, None], current[:, col_start:col_start + NB], 0.0)
        gram_sum = matmul(panel_cols.T, panel_cols)
        chol_low = jnp.linalg.cholesky(gram_sum)
        q_basis = jax.scipy.linalg.solve_triangular(chol_low, panel_cols.T, lower=True).T
        top_block = q_basis[row_start:row_start + NB]
        unit_lower, upper_tri, sign_diag = lu_signed(top_block)
        solved = jax.scipy.linalg.solve_triangular(upper_tri.T, q_basis.T, lower=True).T
        rel_pos = row_ids - row_start
        in_top = (rel_pos >= 0) & (rel_pos < NB)
        lower_rows = jnp.take(unit_lower, jnp.clip(rel_pos, 0, NB - 1), axis=0)
        refl = jnp.where(in_top[:, None], lower_rows, jnp.where((rel_pos < 0)[:, None], 0.0, solved))
        scaled = upper_tri * sign_diag[None, :]
        t_factor = jax.scipy.linalg.solve_triangular(unit_lower, scaled.T, lower=True, unit_diagonal=True).T
        x_rows = matmul(current, matmul(refl, t_factor))
        inner_prod = matmul(refl.T, x_rows)
        w_rows = x_rows - 0.5 * matmul(refl, matmul(t_factor.T, inner_prod))
        current = current - matmul(refl, w_rows.T) - matmul(w_rows, refl.T)
        all_refl.append(refl)
        all_prod.append(w_rows)
    return (current, jnp.stack(all_refl), jnp.stack(all_prod))
```

```python
import functools

import jax
import jax.numpy as jnp
from jax import lax
from jax.experimental import pallas as pl
from jax.experimental.pallas import tpu as pltpu
from jax.sharding import PartitionSpec as P

NB = 256
STRIP = 16


def exact(left, right, dims=((1,), (0,))):
    return lax.dot_general(
        left, right, (dims, ((), ())),
        precision=lax.Precision.HIGHEST, preferred_element_type=jnp.float32,
    )


def split3(left, right, dims=((1,), (0,))):
    return lax.dot_general(
        left, right, (dims, ((), ())),
        precision=lax.Precision.HIGH, preferred_element_type=jnp.float32,
    )


def eliminate(work, held, signed, strip):
    n = work.shape[0]
    lane = lax.broadcasted_iota(jnp.int32, (1, n), 1)
    lanes = lax.broadcasted_iota(jnp.int32, (strip, n), 1)
    subs = lax.broadcasted_iota(jnp.int32, (strip, n), 0)
    signs = jnp.zeros((1, n), jnp.float32)
    held[...] = jnp.zeros_like(held)
    done = []
    for first in range(0, n, strip):
        rows = work[first : first + strip, :]
        forward = rows
        for step in range(strip):
            at = first + step
            row = rows[step : step + 1, :]
            pivot = row[:, at : at + 1]
            if signed:
                sign = jnp.where(pivot >= 0, 1.0, -1.0).astype(jnp.float32)
                pivot = pivot + sign
                signs = jnp.where(lane == at, sign, signs)
            inverse = 1.0 / pivot
            forward = jnp.where(subs == step, jnp.where(lane == at, pivot, row), forward)
            scaled = jnp.where(lane == at, inverse, row * inverse)
            column = rows[:, at : at + 1]
            rest = jnp.where(lanes == at, 0.0, rows) - column * scaled
            rows = jnp.where(subs == step, scaled, rest)
        done.append(forward)
        after = first + strip
        if after < n:
            held[first:after, :] = rows
            below = work[after:, :]
            inside = (lane >= first) & (lane < after)
            lead = jnp.where(inside, below, 0.0)
            work[after:, :] = jnp.where(inside, 0.0, below) - exact(lead, held[...])
            held[first:after, :] = jnp.zeros((strip, n), jnp.float32)
    return jnp.concatenate(done, axis=0), signs


def factor_kernel(strip, gram_ref, top_ref, rinv_ref, lower_ref, linv_ref, uinv_ref, sign_ref,
                  work, held):
    n = gram_ref.shape[0]
    rows = lax.broadcasted_iota(jnp.int32, (n, n), 0)
    cols = lax.broadcasted_iota(jnp.int32, (n, n), 1)
    eye = jnp.where(rows == cols, 1.0, 0.0).astype(jnp.float32)
    work[...] = gram_ref[...]
    packed, _ = eliminate(work, held, False, strip)
    diag = jnp.sum(packed * eye, axis=1, keepdims=True)
    unit_inv = jnp.where(rows > cols, packed, eye)
    chol_inv = unit_inv * (1.0 / jnp.sqrt(diag))
    rinv_ref[...] = chol_inv.T
    top = exact(top_ref[...], rinv_ref[...])
    work[...] = top
    packed, signs = eliminate(work, held, True, strip)
    sign_ref[...] = signs
    linv_ref[...] = jnp.where(rows > cols, packed, eye)
    upper = jnp.where(rows <= cols, packed, 0.0)
    uinv_ref[...] = eye / jnp.sum(packed * eye, axis=1, keepdims=True)
    size = 1
    while size < n:
        mask = ((rows ^ cols) // size == 1) & (cols > rows)
        part = jnp.where(mask, upper, 0.0)
        held_inv = uinv_ref[...]
        uinv_ref[...] = held_inv - exact(exact(held_inv, part), held_inv)
        size *= 2
    low = exact(top + eye * signs, uinv_ref[...])
    lower_ref[...] = jnp.where(rows > cols, low, eye)


def factor(gram, top):
    n = gram.shape[0]
    square = jax.ShapeDtypeStruct((n, n), jnp.float32)
    return pl.pallas_call(
        functools.partial(factor_kernel, STRIP),
        out_shape=[square, square, square, square, jax.ShapeDtypeStruct((1, n), jnp.float32)],
        in_specs=[pl.BlockSpec(memory_space=pltpu.VMEM)] * 2,
        out_specs=[pl.BlockSpec(memory_space=pltpu.VMEM)] * 5,
        scratch_shapes=[pltpu.VMEM((n, n), jnp.float32), pltpu.VMEM((n, n), jnp.float32)],
        compiler_params=pltpu.CompilerParams(vmem_limit_bytes=16 * 1024 * 1024),
        cost_estimate=pl.CostEstimate(flops=20_000_000_000, bytes_accessed=2_000_000, transcendentals=0),
        name="factor",
    )(gram, top)


def body(matrix):
    row_count, col_count = matrix.shape
    n_row, n_col = lax.axis_size("row"), lax.axis_size("col")
    both = ("row", "col")
    share = row_count // n_col
    r, c = lax.axis_index("row"), lax.axis_index("col")
    first = NB
    head = matrix[: 2 * NB, :].T
    col_ids = c * col_count + jnp.arange(col_count)
    panel_own = jnp.where((col_ids >= first)[:, None], head[:, :NB], 0.0)
    next_own = head[:, NB:]
    pieces = [panel_own[k * share : (k + 1) * share] for k in range(n_row)]
    nexts = [next_own[k * share : (k + 1) * share] for k in range(n_row)]
    by_row = sum(
        lax.ppermute(pieces[k], both, [(j, j * n_row + k) for j in range(n_col)])
        for k in range(n_row)
    )

    def to_column_order(parts):
        total = jnp.where(r == 0, parts[0], 0.0)
        for k in range(1, n_row):
            total = total + lax.ppermute(parts[k], "row", [(0, k)])
        return total

    by_col = to_column_order(pieces)
    next_by_col = to_column_order(nexts)
    corner = (r == 0) & (c == 0)
    gram = exact(by_row, by_row, ((0,), (0,)))
    tops = jnp.where(corner, jnp.concatenate([panel_own[first : first + NB], next_own[first : first + NB]]), 0.0)
    small = lax.psum(jnp.concatenate([gram, tops]), both)
    gram_sum, top, next_top = small[:NB], small[NB : 2 * NB], small[2 * NB :]
    rinv, unit_lower, linv, uinv, signs = factor(gram_sum, top)

    panel_rows = lax.all_gather(by_row, "col", axis=0, tiled=True)
    panel_cols = lax.all_gather(by_col, "row", axis=0, tiled=True)
    y_part = split3(matrix, panel_rows, ((0,), (0,)))
    y_top = jnp.where(c == 0, y_part[first : first + NB], 0.0)
    inner = exact(panel_cols, y_part, ((0,), (0,)))
    later, gram_sum = lax.optimization_barrier((jnp.concatenate([inner, y_top]), gram_sum))
    small = lax.psum(later, both)
    inner_sum, y_top = small[:NB], small[NB:]
    y_share = lax.psum_scatter(y_part, "row", scatter_dimension=0, tiled=True)

    scaled_inv = rinv * signs
    x_share = exact(exact(y_share, scaled_inv) + next_by_col, linv, ((1,), (1,)))
    x_share_row = lax.ppermute(
        x_share, both, [(k * n_col + j, j * n_row + k) for k in range(n_row) for j in range(n_col)]
    )
    x_rows = lax.all_gather(x_share_row, "col", axis=0, tiled=True)
    x_cols = lax.all_gather(x_share, "row", axis=0, tiled=True)

    cross = exact(y_top, scaled_inv)
    middle = exact(scaled_inv, exact(inner_sum, scaled_inv), ((0,), (0,))) + cross + cross.T + next_top
    half = 0.5 * exact(linv, exact(middle, linv, ((1,), (1,))))
    shape = exact(rinv, uinv)

    def reflectors(panel, start):
        out = split3(panel, shape)
        rel = start + jnp.arange(panel.shape[0]) - first
        top_rows = jnp.zeros_like(out[: 2 * NB]).at[first:].set(unit_lower)
        in_top = (start == 0) & (rel < NB)
        padded = jnp.concatenate([top_rows, out[2 * NB :]])
        return jnp.where(in_top[:, None], padded, out)

    refl_rows = reflectors(panel_rows, r * row_count)
    refl_cols = reflectors(panel_cols, c * col_count)
    w_rows = x_rows - split3(refl_rows, half)
    w_cols = x_cols - split3(refl_cols, half)
    left = jnp.concatenate([refl_rows, w_rows], axis=1)
    right = jnp.concatenate([w_cols, refl_cols], axis=1)
    updated = matrix - split3(left, right, ((1,), (1,)))
    v_out = lax.dynamic_slice_in_dim(refl_rows, c * share, share, 0)
    w_out = lax.dynamic_slice_in_dim(w_rows, c * share, share, 0)
    return updated, v_out[None], w_out[None]


def solution(mesh):
    return jax.shard_map(
        body,
        mesh=mesh,
        in_specs=(P("row", "col"),),
        out_specs=(P("row", "col"), P(None, ("row", "col"), None), P(None, ("row", "col"), None)),
        check_vma=False,
    )
```
